32 devices in a mesh: rows: 4 (over x, core), feat: 8 (over z, y).
Axes of the slice: x: 2, y: 2, z: 4, core: 2. Of those that a mesh axis runs over, the one named last changes fastest.
Arguments:
- embeddings: bfloat16 [512, 1024], P(('rows', 'feat')), may hold values from -12 to 12
- freqs: bfloat16 [1024, 65536], P(None, 'feat'), may hold values from -0.1875 to 0.1875
- phases: float32 [65536], P('feat'), may hold values from 0 to 6.2831855
- sketch: bfloat16 [65536, 256], P('feat'), may hold values from -0.0234375 to 0.0234375
Outputs:
- basis: float32 [512, 256], P(('rows', 'feat'))
- coeffs: float32 [256, 65536], P(None, 'feat')
The draws below stay inside these ranges and needn't reach their ends.
All inputs are finite; a program needn't handle non-finite values.
Results may differ from the reference program's by a relative error of at most 0.0048.
Values may be sent and summed in bfloat16 or wider, within the bound.
A program may use at most 128 MiB of HBM per device.

```python
import jax
import jax.numpy as jnp
from jax import lax

D = 1024
F = 65536
K = 256
ROWS = 512
N_FEAT = 8


def steps_of(rng, shape, pieces, smallest, top_value):
    level = 1.0
    for dim, parts in pieces:
        heights = jax.random.uniform(jax.random.fold_in(jax.random.fold_in(rng, 6), dim), (parts,), jnp.float32, smallest / len(pieces), top_value / len(pieces))
        level = level * jnp.repeat(jnp.exp(heights), shape[dim] // parts).reshape((-1,) + (1,) * (len(shape) - 1 - dim))
    return level


def scatter_about(own_key, shape, deviation, reach, cuts=(), kind=jnp.bfloat16):
    drawn = deviation * jax.random.normal(own_key, shape, jnp.float32)
    if cuts:
        drawn = drawn * steps_of(own_key, shape, cuts, -0.22, 0.18)
    return jnp.clip(drawn, -reach, reach).astype(kind)


def setup_inputs(seed: int = 0) -> dict:
    key_list = jax.random.split(jax.random.key(seed), 5)
    embeddings = scatter_about(key_list[0], (ROWS, D), 2.0, 12.0, ((0, 32),))
    freqs = scatter_about(key_list[1], (D, F), D ** -0.5, 0.1875, ((1, 8),))
    phases = jnp.clip(6.2831855 * jax.random.uniform(key_list[2], (F,), jnp.float32) ** steps_of(key_list[2], (F,), ((0, 8),), -0.2, 0.2), 0.0, 6.2831855)
    sketch = scatter_about(key_list[3], (F, K), F ** -0.5, 0.0234375, ((0, 8),))
    return {"embeddings": embeddings, "freqs": freqs, "phases": phases, "sketch": sketch}


def reference(embeddings, freqs, phases, sketch):
    width = F // N_FEAT

    def featurize_block(column):
        freq_block = lax.dynamic_slice_in_dim(freqs, column * width, width, 1)
        phase_block = lax.dynamic_slice_in_dim(phases, column * width, width, 0)
        sketch_block = lax.dynamic_slice_in_dim(sketch, column * width, width, 0)
        features = jnp.cos(jnp.dot(embeddings.astype(jnp.float32), freq_block.astype(jnp.float32), preferred_element_type=jnp.float32) + phase_block).astype(jnp.bfloat16)
        partial_value = jnp.dot(features.astype(jnp.float32), sketch_block.astype(jnp.float32), preferred_element_type=jnp.float32)
        return (features, partial_value)
    feature_blocks, partials = lax.map(featurize_block, jnp.arange(N_FEAT, dtype=jnp.int32))
    sketched = jnp.sum(partials, axis=0)
    gram_matrix = jnp.dot(sketched.T, sketched, precision=lax.Precision.HIGHEST) / ROWS
    factor = jnp.linalg.cholesky(gram_matrix)
    basis = jax.scipy.linalg.solve_triangular(factor, sketched.T, lower=True).T
    basis_half = basis.astype(jnp.bfloat16)

    def project_block(features):
        return lax.dot_general(basis_half.astype(jnp.float32), features.astype(jnp.float32), (((0,), (0,)), ((), ())), preferred_element_type=jnp.float32)
    projected = lax.map(project_block, feature_blocks)
    coeffs = jnp.transpose(projected, (1, 0, 2)).reshape(K, F) / ROWS
    return (basis, coeffs)
```

```python
import functools

import jax
import jax.numpy as jnp
from jax import lax
from jax.experimental import pallas as pl
from jax.experimental.pallas import tpu as pltpu
from jax.sharding import PartitionSpec as P

MESH = pl.DeviceIdType.MESH
MIB = 1 << 20

INV_TAU = 0.15915494309189535
TAU_HI = 6.283203125
TAU_LO = -1.7817820414e-05
HALF_PI = 1.5707963267948966
ROUND = 12582912.0


def cosine(x):
    n = (x * INV_TAU + ROUND) - ROUND
    r = (x - n * TAU_HI) - n * TAU_LO
    w = HALF_PI - jnp.abs(r)
    z = w * w
    p = -2.3889859e-08
    p = p * z + 2.7525562e-06
    p = p * z - 1.9840874e-04
    p = p * z + 8.3333310e-03
    p = p * z - 1.6666667e-01
    return w + w * (z * p)


def peers(feats):
    r, f = lax.axis_index("rows"), lax.axis_index("feat")
    x, c = r // 2, r % 2
    sib = x * 2 + (1 - c)
    across = (1 - x) * 2 + c
    both = (1 - x) * 2 + (1 - c)
    return r, f, sib, across, both


def entry_barrier(feats):
    r, f, sib, across, _ = peers(feats)
    barrier = pltpu.get_barrier_semaphore()
    targets = [(r, lax.rem(f + k, feats)) for k in range(1, feats)]
    targets += [(sib, f), (across, f)]
    for target in targets:
        pl.semaphore_signal(barrier, inc=1, device_id=target, device_id_type=MESH)
    pl.semaphore_wait(barrier, feats + 1)


def spread(feats, rows, out_ref, send_sem, recv_sem):
    r, f, sib, across, both = peers(feats)

    def chunk(rr, ff):
        start = pl.multiple_of((rr * feats + ff) * rows, rows)
        return out_ref.at[pl.ds(start, rows)]

    sends = []

    def copy_of(rr, ff, target, slot):
        return pltpu.make_async_remote_copy(
            src_ref=chunk(rr, ff),
            dst_ref=chunk(rr, ff),
            send_sem=send_sem.at[slot],
            recv_sem=recv_sem.at[rr * feats + ff],
            device_id=target,
            device_id_type=MESH,
        )

    def send(rr, ff, target):
        copy = copy_of(rr, ff, target, len(sends))
        copy.start()
        sends.append(copy)

    def arrive(rr, ff):
        copy_of(rr, ff, (sib, f), 0).wait_recv()

    send(r, f, (across, f))
    for k in range(1, feats):
        send(r, f, (r, lax.rem(f + k, feats)))
    send(r, f, (sib, f))
    for k in range(1, feats):
        ff = lax.rem(f - k + feats, feats)
        arrive(r, ff)
        send(r, ff, (across, f))
        send(r, ff, (sib, f))
    for k in range(feats):
        ff = lax.rem(f - k + feats, feats)
        arrive(across, ff)
        send(across, ff, (sib, f))
    for k in range(feats):
        ff = lax.rem(f - k + feats, feats)
        arrive(sib, ff)
        arrive(both, ff)
    for copy in sends:
        copy.wait_send()


def gather_kernel(feats, x_ref, out_ref, send_sem, recv_sem):
    rows = x_ref.shape[0]
    r, f, *_ = peers(feats)
    entry_barrier(feats)
    start = pl.multiple_of((r * feats + f) * rows, rows)
    out_ref[pl.ds(start, rows), :] = x_ref[...]
    spread(feats, rows, out_ref, send_sem, recv_sem)


def gather_rows(x, feats, parts):
    rows, width = x.shape
    return pl.pallas_call(
        functools.partial(gather_kernel, feats),
        out_shape=jax.ShapeDtypeStruct((rows * feats * parts, width), x.dtype),
        in_specs=[pl.BlockSpec(memory_space=pltpu.VMEM)],
        out_specs=pl.BlockSpec(memory_space=pltpu.VMEM),
        scratch_shapes=[
            pltpu.SemaphoreType.DMA((feats * parts,)),
            pltpu.SemaphoreType.DMA((feats * parts,)),
        ],
        compiler_params=pltpu.CompilerParams(collective_id=0, has_side_effects=True),
    )(x)


def sum_kernel(feats, part_ref, feat_ref, out_ref, other_ref, own, pair, inbox,
               send_sem, recv_sem, pair_send, pair_recv, box_send, box_recv,
               feat_send, feat_recv):
    total = part_ref.shape[0]
    block = total // 4
    rows = block // feats
    r, f, sib, across, _ = peers(feats)
    entry_barrier(feats)

    def part(rr):
        return part_ref.at[pl.ds(pl.multiple_of(rr * block, block), block)]

    exchange = pltpu.make_async_remote_copy(
        src_ref=part(sib), dst_ref=pair, send_sem=pair_send, recv_sem=pair_recv,
        device_id=(sib, f), device_id_type=MESH,
    )
    exchange.start()
    features = pltpu.make_async_remote_copy(
        src_ref=feat_ref, dst_ref=other_ref, send_sem=feat_send, recv_sem=feat_recv,
        device_id=(sib, f), device_id_type=MESH,
    )
    exchange.wait()
    features.start()
    mine = pl.ds(pl.multiple_of(r * block, block), block)
    own[...] = part_ref[mine, :] + pair[...]

    sends = []
    for k in range(1, feats):
        ff = lax.rem(f + k, feats)
        copy = pltpu.make_async_remote_copy(
            src_ref=own.at[pl.ds(pl.multiple_of(ff * rows, rows), rows)],
            dst_ref=inbox.at[k - 1],
            send_sem=box_send.at[k - 1],
            recv_sem=box_recv.at[k - 1],
            device_id=(r, ff),
            device_id_type=MESH,
        )
        copy.start()
        sends.append(copy)
    acc = own[pl.ds(pl.multiple_of(f * rows, rows), rows), :]
    for k in range(1, feats):
        sends[k - 1].wait_recv()
        acc = acc + inbox[k - 1]
    start = pl.multiple_of((r * feats + f) * rows, rows)
    out_ref[pl.ds(start, rows), :] = acc
    spread(feats, rows, out_ref, send_sem, recv_sem)
    for copy in sends:
        copy.wait_send()
    features.wait()


def sum_and_swap(partial, features, feats):
    total, k = partial.shape
    parts = 4
    dma = pltpu.SemaphoreType.DMA
    return pl.pallas_call(
        functools.partial(sum_kernel, feats),
        out_shape=(
            jax.ShapeDtypeStruct((total, k), jnp.float32),
            jax.ShapeDtypeStruct(features.shape, features.dtype),
        ),
        in_specs=[
            pl.BlockSpec(memory_space=pltpu.VMEM),
            pl.BlockSpec(memory_space=pl.ANY),
        ],
        out_specs=(
            pl.BlockSpec(memory_space=pltpu.VMEM),
            pl.BlockSpec(memory_space=pl.ANY),
        ),
        scratch_shapes=[
            pltpu.VMEM((total // parts, k), jnp.float32),
            pltpu.VMEM((total // parts, k), jnp.float32),
            pltpu.VMEM((feats - 1, total // parts // feats, k), jnp.float32),
            dma((feats * parts,)),
            dma((feats * parts,)),
            dma(()),
            dma(()),
            dma((feats - 1,)),
            dma((feats - 1,)),
            dma(()),
            dma(()),
        ],
        compiler_params=pltpu.CompilerParams(collective_id=1, has_side_effects=True),
    )(partial, features)


def feature_kernel(core_ref, emb_ref, freq_ref, phase_ref, sketch_ref, feat_ref, part_ref):
    mixed = jnp.dot(emb_ref[...], freq_ref[...], preferred_element_type=jnp.float32)
    value = cosine(mixed + phase_ref[...]).astype(jnp.bfloat16)
    feat_ref[...] = value
    term = jnp.dot(value, sketch_ref[...], preferred_element_type=jnp.float32)

    @pl.when(pl.program_id(0) == 0)
    def _():
        part_ref[...] = term

    @pl.when(pl.program_id(0) > 0)
    def _():
        part_ref[...] += term


def featurize(core, emb, freqs, phases, sketch, tile=512):
    total, depth = emb.shape
    width = freqs.shape[1] // 2
    k = sketch.shape[1]
    steps = width // tile
    return pl.pallas_call(
        feature_kernel,
        grid_spec=pltpu.PrefetchScalarGridSpec(
            num_scalar_prefetch=1,
            grid=(steps,),
            in_specs=[
                pl.BlockSpec((total, depth), lambda i, c: (0, 0)),
                pl.BlockSpec((depth, tile), lambda i, c: (0, c[0] * steps + i)),
                pl.BlockSpec((1, tile), lambda i, c: (0, c[0] * steps + i)),
                pl.BlockSpec((tile, k), lambda i, c: (c[0] * steps + i, 0)),
            ],
            out_specs=[
                pl.BlockSpec((total, tile), lambda i, c: (0, i)),
                pl.BlockSpec((total, k), lambda i, c: (0, 0)),
            ],
        ),
        out_shape=(
            jax.ShapeDtypeStruct((total, width), jnp.bfloat16),
            jax.ShapeDtypeStruct((total, k), jnp.float32),
        ),
        compiler_params=pltpu.CompilerParams(vmem_limit_bytes=32 * MIB),
    )(core, emb, freqs, phases.reshape(1, -1), sketch)


def coeff_kernel(scale, half, core_ref, basis_ref, own_ref, other_ref, out_ref):
    step = pl.program_id(0)

    @pl.when(step < half)
    def _():
        out_ref[...] = scale * jnp.dot(
            basis_ref[...], own_ref[...], preferred_element_type=jnp.float32
        )

    @pl.when(step >= half)
    def _():
        out_ref[...] = scale * jnp.dot(
            basis_ref[...], other_ref[...], preferred_element_type=jnp.float32
        )


def project(core, basis_t, own, other, tile=1024):
    k, total = basis_t.shape
    width = own.shape[1]
    half = width // tile
    return pl.pallas_call(
        functools.partial(coeff_kernel, 1.0 / total, half),
        grid_spec=pltpu.PrefetchScalarGridSpec(
            num_scalar_prefetch=1,
            grid=(2 * half,),
            in_specs=[
                pl.BlockSpec((k, total), lambda i, c: (0, 0)),
                pl.BlockSpec((total, tile), lambda i, c: (0, jnp.minimum(i, half - 1))),
                pl.BlockSpec((total, tile), lambda i, c: (0, jnp.maximum(i - half, 0))),
            ],
            out_specs=pl.BlockSpec(
                (k, tile),
                lambda i, c: (0, jnp.where(i < half, c[0], 1 - c[0]) * half + i % half),
            ),
        ),
        out_shape=jax.ShapeDtypeStruct((k, 2 * width), jnp.float32),
        compiler_params=pltpu.CompilerParams(vmem_limit_bytes=32 * MIB),
    )(core, basis_t, own, other)


def fused(embeddings, freqs, phases, sketch):
    rows_dev = embeddings.shape[0]
    feats, parts = lax.axis_size("feat"), lax.axis_size("rows")
    row_count = rows_dev * feats * parts
    r, f = lax.axis_index("rows"), lax.axis_index("feat")
    core = jnp.reshape(r % 2, (1,)).astype(jnp.int32)
    emb = gather_rows(embeddings, feats, parts)
    own, partial = featurize(core, emb, freqs, phases, sketch)
    sketched, other = sum_and_swap(partial, own, feats)
    gram = jnp.dot(sketched.T, sketched, precision=lax.Precision.HIGHEST) / row_count
    factor = jnp.linalg.cholesky(gram)
    basis_t = jax.scipy.linalg.solve_triangular(factor, sketched.T, lower=True)
    start = (r * feats + f) * rows_dev
    basis = lax.dynamic_slice_in_dim(basis_t, start, rows_dev, 1).T
    coeffs = project(core, basis_t.astype(jnp.bfloat16), own, other)
    return basis, coeffs


def general(embeddings, freqs, phases, sketch):
    rows_dev = embeddings.shape[0]
    row_count = rows_dev * lax.axis_size("feat") * lax.axis_size("rows")
    mixed = jnp.dot(
        lax.all_gather(embeddings, "feat", axis=0, tiled=True),
        freqs,
        preferred_element_type=jnp.float32,
    )
    features = jnp.cos(mixed + phases).astype(jnp.bfloat16)
    owned_rows = lax.psum_scatter(
        jnp.dot(features, sketch, preferred_element_type=jnp.float32),
        "feat",
        scatter_dimension=0,
        tiled=True,
    )
    local_gram = jnp.dot(owned_rows.T, owned_rows, precision=lax.Precision.HIGHEST)
    gram_matrix = lax.psum(local_gram, ("rows", "feat")) / row_count
    factor = jnp.linalg.cholesky(gram_matrix)
    basis = jax.scipy.linalg.solve_triangular(factor, owned_rows.T, lower=True).T
    block_basis = lax.all_gather(basis.astype(jnp.bfloat16), "feat", axis=0, tiled=True)
    partial_value = lax.dot_general(
        block_basis, features, (((0,), (0,)), ((), ())), preferred_element_type=jnp.float32
    )
    coeffs = lax.psum(partial_value, "rows") / row_count
    return (basis, coeffs)


def per_device(embeddings, freqs, phases, sketch):
    row_count = embeddings.shape[0] * lax.axis_size("feat") * lax.axis_size("rows")
    small = row_count <= 1024 and lax.axis_size("rows") == 4 and freqs.shape[1] % 2048 == 0
    form = fused if small else general
    return form(embeddings, freqs, phases, sketch)


def solution(mesh):
    placed = (P(("rows", "feat"), None), P(None, "feat"), P("feat"), P("feat", None))
    return jax.shard_map(
        per_device,
        mesh=mesh,
        in_specs=placed,
        out_specs=(P(("rows", "feat"), None), P(None, "feat")),
        check_vma=False,
    )
```

```python
import functools

import jax
import jax.numpy as jnp
from jax import lax
from jax.experimental import pallas as pl
from jax.experimental.pallas import tpu as pltpu
from jax.sharding import PartitionSpec as P

MESH = pl.DeviceIdType.MESH
MIB = 1 << 20

INV_TAU = 0.15915494309189535
TAU_HI = 6.283203125
TAU_LO = -1.7817820414e-05
HALF_PI = 1.5707963267948966
ROUND = 12582912.0


def cosine(x):
    n = (x * INV_TAU + ROUND) - ROUND
    r = (x - n * TAU_HI) - n * TAU_LO
    w = HALF_PI - jnp.abs(r)
    z = w * w
    p = -2.3889859e-08
    p = p * z + 2.7525562e-06
    p = p * z - 1.9840874e-04
    p = p * z + 8.3333310e-03
    p = p * z - 1.6666667e-01
    return w + w * (z * p)


def peers(feats):
    r, f = lax.axis_index("rows"), lax.axis_index("feat")
    x, c = r // 2, r % 2
    sib = x * 2 + (1 - c)
    across = (1 - x) * 2 + c
    both = (1 - x) * 2 + (1 - c)
    return r, f, sib, across, both


def entry_barrier(feats):
    r, f, sib, across, _ = peers(feats)
    barrier = pltpu.get_barrier_semaphore()
    targets = [(r, lax.rem(f + k, feats)) for k in range(1, feats)]
    targets += [(sib, f), (across, f)]
    for target in targets:
        pl.semaphore_signal(barrier, inc=1, device_id=target, device_id_type=MESH)
    pl.semaphore_wait(barrier, feats + 1)


def spread(feats, rows, out_ref, send_sem, recv_sem):
    r, f, sib, across, both = peers(feats)

    def chunk(rr, ff):
        start = pl.multiple_of((rr * feats + ff) * rows, rows)
        return out_ref.at[pl.ds(start, rows)]

    sends = []

    def copy_of(rr, ff, target, slot):
        return pltpu.make_async_remote_copy(
            src_ref=chunk(rr, ff),
            dst_ref=chunk(rr, ff),
            send_sem=send_sem.at[slot],
            recv_sem=recv_sem.at[rr * feats + ff],
            device_id=target,
            device_id_type=MESH,
        )

    def send(rr, ff, target):
        copy = copy_of(rr, ff, target, len(sends))
        copy.start()
        sends.append(copy)

    def arrive(rr, ff):
        copy_of(rr, ff, (sib, f), 0).wait_recv()

    send(r, f, (across, f))
    for k in range(1, feats):
        send(r, f, (r, lax.rem(f + k, feats)))
    send(r, f, (sib, f))
    for k in range(1, feats):
        ff = lax.rem(f - k + feats, feats)
        arrive(r, ff)
        send(r, ff, (across, f))
        send(r, ff, (sib, f))
    for k in range(feats):
        ff = lax.rem(f - k + feats, feats)
        arrive(across, ff)
        send(across, ff, (sib, f))
    for k in range(feats):
        ff = lax.rem(f - k + feats, feats)
        arrive(sib, ff)
        arrive(both, ff)
    for copy in sends:
        copy.wait_send()


def gather_kernel(feats, x_ref, out_ref, send_sem, recv_sem):
    rows = x_ref.shape[0]
    r, f, *_ = peers(feats)
    entry_barrier(feats)
    start = pl.multiple_of((r * feats + f) * rows, rows)
    out_ref[pl.ds(start, rows), :] = x_ref[...]
    spread(feats, rows, out_ref, send_sem, recv_sem)


def gather_rows(x, feats, parts):
    rows, width = x.shape
    return pl.pallas_call(
        functools.partial(gather_kernel, feats),
        out_shape=jax.ShapeDtypeStruct((rows * feats * parts, width), x.dtype),
        in_specs=[pl.BlockSpec(memory_space=pltpu.VMEM)],
        out_specs=pl.BlockSpec(memory_space=pltpu.VMEM),
        scratch_shapes=[
            pltpu.SemaphoreType.DMA((feats * parts,)),
            pltpu.SemaphoreType.DMA((feats * parts,)),
        ],
        compiler_params=pltpu.CompilerParams(collective_id=0, has_side_effects=True),
    )(x)


def sum_kernel(feats, part_ref, feat_ref, out_ref, other_ref, own, pair, inbox,
               send_sem, recv_sem, pair_send, pair_recv, box_send, box_recv,
               feat_send, feat_recv):
    total = part_ref.shape[0]
    block = total // 4
    rows = block // feats
    r, f, sib, across, _ = peers(feats)
    entry_barrier(feats)

    def part(rr):
        return part_ref.at[pl.ds(pl.multiple_of(rr * block, block), block)]

    exchange = pltpu.make_async_remote_copy(
        src_ref=part(sib), dst_ref=pair, send_sem=pair_send, recv_sem=pair_recv,
        device_id=(sib, f), device_id_type=MESH,
    )
    exchange.start()
    features = pltpu.make_async_remote_copy(
        src_ref=feat_ref, dst_ref=other_ref, send_sem=feat_send, recv_sem=feat_recv,
        device_id=(sib, f), device_id_type=MESH,
    )
    exchange.wait()
    features.start()
    mine = pl.ds(pl.multiple_of(r * block, block), block)
    own[...] = part_ref[mine, :] + pair[...]

    sends = []
    for k in range(1, feats):
        ff = lax.rem(f + k, feats)
        copy = pltpu.make_async_remote_copy(
            src_ref=own.at[pl.ds(pl.multiple_of(ff * rows, rows), rows)],
            dst_ref=inbox.at[k - 1],
            send_sem=box_send.at[k - 1],
            recv_sem=box_recv.at[k - 1],
            device_id=(r, ff),
            device_id_type=MESH,
        )
        copy.start()
        sends.append(copy)
    acc = own[pl.ds(pl.multiple_of(f * rows, rows), rows), :]
    for k in range(1, feats):
        sends[k - 1].wait_recv()
        acc = acc + inbox[k - 1]
    start = pl.multiple_of((r * feats + f) * rows, rows)
    out_ref[pl.ds(start, rows), :] = acc
    spread(feats, rows, out_ref, send_sem, recv_sem)
    for copy in sends:
        copy.wait_send()
    features.wait()


def sum_and_swap(partial, features, feats):
    total, k = partial.shape
    parts = 4
    dma = pltpu.SemaphoreType.DMA
    return pl.pallas_call(
        functools.partial(sum_kernel, feats),
        out_shape=(
            jax.ShapeDtypeStruct((total, k), jnp.float32),
            jax.ShapeDtypeStruct(features.shape, features.dtype),
        ),
        in_specs=[
            pl.BlockSpec(memory_space=pltpu.VMEM),
            pl.BlockSpec(memory_space=pl.ANY),
        ],
        out_specs=(
            pl.BlockSpec(memory_space=pltpu.VMEM),
            pl.BlockSpec(memory_space=pl.ANY),
        ),
        scratch_shapes=[
            pltpu.VMEM((total // parts, k), jnp.float32),
            pltpu.VMEM((total // parts, k), jnp.float32),
            pltpu.VMEM((feats - 1, total // parts // feats, k), jnp.float32),
            dma((feats * parts,)),
            dma((feats * parts,)),
            dma(()),
            dma(()),
            dma((feats - 1,)),
            dma((feats - 1,)),
            dma(()),
            dma(()),
        ],
        compiler_params=pltpu.CompilerParams(collective_id=1, has_side_effects=True, vmem_limit_bytes=60 * MIB),
    )(partial, features)


def feature_kernel(core_ref, emb_ref, freq_ref, phase_ref, sketch_ref, feat_ref, part_ref):
    mixed = jnp.dot(emb_ref[...], freq_ref[...], preferred_element_type=jnp.float32)
    value = cosine(mixed + phase_ref[...]).astype(jnp.bfloat16)
    feat_ref[...] = value
    term = jnp.dot(value, sketch_ref[...], preferred_element_type=jnp.float32)

    @pl.when(pl.program_id(0) == 0)
    def _():
        part_ref[...] = term

    @pl.when(pl.program_id(0) > 0)
    def _():
        part_ref[...] += term


def featurize(core, emb, freqs, phases, sketch, tile=512):
    total, depth = emb.shape
    width = freqs.shape[1] // 2
    k = sketch.shape[1]
    steps = width // tile
    return pl.pallas_call(
        feature_kernel,
        grid_spec=pltpu.PrefetchScalarGridSpec(
            num_scalar_prefetch=1,
            grid=(steps,),
            in_specs=[
                pl.BlockSpec((total, depth), lambda i, c: (0, 0)),
                pl.BlockSpec((depth, tile), lambda i, c: (0, c[0] * steps + i)),
                pl.BlockSpec((1, tile), lambda i, c: (0, c[0] * steps + i)),
                pl.BlockSpec((tile, k), lambda i, c: (c[0] * steps + i, 0)),
            ],
            out_specs=[
                pl.BlockSpec((total, tile), lambda i, c: (0, i)),
                pl.BlockSpec((total, k), lambda i, c: (0, 0)),
            ],
        ),
        out_shape=(
            jax.ShapeDtypeStruct((total, width), jnp.bfloat16),
            jax.ShapeDtypeStruct((total, k), jnp.float32),
        ),
        compiler_params=pltpu.CompilerParams(vmem_limit_bytes=60 * MIB),
    )(core, emb, freqs, phases.reshape(1, -1), sketch)


def coeff_kernel(scale, half, core_ref, basis_ref, own_ref, other_ref, out_ref):
    step = pl.program_id(0)

    @pl.when(step < half)
    def _():
        out_ref[...] = scale * jnp.dot(
            basis_ref[...], own_ref[...], preferred_element_type=jnp.float32
        )

    @pl.when(step >= half)
    def _():
        out_ref[...] = scale * jnp.dot(
            basis_ref[...], other_ref[...], preferred_element_type=jnp.float32
        )


def project(core, basis_t, own, other, tile=1024):
    k, total = basis_t.shape
    width = own.shape[1]
    half = width // tile
    return pl.pallas_call(
        functools.partial(coeff_kernel, 1.0 / total, half),
        grid_spec=pltpu.PrefetchScalarGridSpec(
            num_scalar_prefetch=1,
            grid=(2 * half,),
            in_specs=[
                pl.BlockSpec((k, total), lambda i, c: (0, 0)),
                pl.BlockSpec((total, tile), lambda i, c: (0, jnp.minimum(i, half - 1))),
                pl.BlockSpec((total, tile), lambda i, c: (0, jnp.maximum(i - half, 0))),
            ],
            out_specs=pl.BlockSpec(
                (k, tile),
                lambda i, c: (0, jnp.where(i < half, c[0], 1 - c[0]) * half + i % half),
            ),
        ),
        out_shape=jax.ShapeDtypeStruct((k, 2 * width), jnp.float32),
        compiler_params=pltpu.CompilerParams(vmem_limit_bytes=60 * MIB),
    )(core, basis_t, own, other)


GROUP = 8
BLOCK = 64
LANES = 128


def eliminate(tile, at):
    groups = BLOCK // GROUP
    m = [tile[g * GROUP:(g + 1) * GROUP, :] for g in range(groups)]
    shape = (GROUP, LANES)
    sub = lax.broadcasted_iota(jnp.int32, shape, 0)
    done = []
    for g0 in range(groups):
        base = at + g0 * GROUP
        col = [
            {g: jnp.broadcast_to(m[g][:, base + t:base + t + 1], shape) for g in range(g0, groups)}
            for t in range(GROUP)
        ]
        row = [jnp.broadcast_to(m[g0][t:t + 1, :], shape) for t in range(GROUP)]
        a = {
            (t, s): jnp.broadcast_to(col[s][g0][t:t + 1, :], shape)
            for t in range(GROUP)
            for s in range(t, GROUP)
        }
        pivots = jnp.zeros(shape, jnp.float32)
        for t in range(GROUP):
            inv = 1.0 / a[t, t]
            pivots = jnp.where(sub == t, a[t, t], pivots)
            for s in range(t + 1, GROUP):
                scaled = a[t, s] * inv
                for u in range(s, GROUP):
                    a[s, u] = a[s, u] - scaled * a[t, u]
                row[s] = row[s] - scaled * row[t]
            for g in range(g0, groups):
                f = col[t][g] * inv
                if g == g0:
                    f = jnp.where(sub > t, f, 0.0)
                for s in range(t + 1, GROUP):
                    col[s][g] = col[s][g] - f * a[t, s]
                m[g] = m[g] - f * row[t]
        done.append(m[g0] * lax.rsqrt(pivots))
    return jnp.concatenate(done, axis=0)


def solve_kernel(scale, sk_ref, basis_ref, half_ref, work):
    k = sk_ref.shape[1]
    exact = dict(preferred_element_type=jnp.float32, precision=lax.Precision.HIGHEST)
    sk = sk_ref[...]
    st = sk.T
    work[:, :k] = jnp.dot(st, sk, **exact) * scale
    work[:, k:] = st
    tile_row = lax.broadcasted_iota(jnp.int32, (BLOCK, LANES), 0)
    tile_lane = lax.broadcasted_iota(jnp.int32, (BLOCK, LANES), 1)
    for j in range(k // BLOCK):
        rows = slice(j * BLOCK, (j + 1) * BLOCK)
        edge = j * BLOCK // LANES * LANES
        at = j * BLOCK - edge
        away = BLOCK - at
        inside = (tile_lane >= at) & (tile_lane < at + BLOCK)
        eye = jnp.where(tile_lane == tile_row + away, 1.0, 0.0)
        tile = jnp.where(inside, work[rows, edge:edge + LANES], eye)
        inverse = jnp.where(inside, 0.0, eliminate(tile, at))
        panel = work[rows, edge:]
        panel = jnp.dot(inverse, jnp.concatenate([panel, panel], axis=0), **exact)
        basis_ref[rows, :] = panel[:, k - edge:]
        after = (j + 1) * BLOCK
        if after < k:
            left = after // LANES * LANES
            wide = panel[:, left - edge:]
            update = lax.dot_general(
                wide[:, :k - left], wide, (((0,), (0,)), ((), ())), **exact
            )
            work[after:, left:] = work[after:, left:] - update[after - left:, :]
    half_ref[...] = basis_ref[...].astype(jnp.bfloat16)


def solve(sketched):
    total, k = sketched.shape
    return pl.pallas_call(
        functools.partial(solve_kernel, 1.0 / total),
        out_shape=(
            jax.ShapeDtypeStruct((k, total), jnp.float32),
            jax.ShapeDtypeStruct((k, total), jnp.bfloat16),
        ),
        in_specs=[pl.BlockSpec(memory_space=pltpu.VMEM)],
        out_specs=(pl.BlockSpec(memory_space=pltpu.VMEM),) * 2,
        scratch_shapes=[pltpu.VMEM((k, k + total), jnp.float32)],
        compiler_params=pltpu.CompilerParams(vmem_limit_bytes=32 * MIB),
    )(sketched)


def fused(embeddings, freqs, phases, sketch):
    rows_dev = embeddings.shape[0]
    feats, parts = lax.axis_size("feat"), lax.axis_size("rows")
    row_count = rows_dev * feats * parts
    r, f = lax.axis_index("rows"), lax.axis_index("feat")
    core = jnp.reshape(r % 2, (1,)).astype(jnp.int32)
    emb = gather_rows(embeddings, feats, parts)
    own, partial = featurize(core, emb, freqs, phases, sketch)
    sketched, other = sum_and_swap(partial, own, feats)
    basis_t, half_t = solve(sketched)
    start = (r * feats + f) * rows_dev
    basis = lax.dynamic_slice_in_dim(basis_t, start, rows_dev, 1).T
    coeffs = project(core, half_t, own, other)
    return basis, coeffs


def general(embeddings, freqs, phases, sketch):
    rows_dev = embeddings.shape[0]
    row_count = rows_dev * lax.axis_size("feat") * lax.axis_size("rows")
    mixed = jnp.dot(
        lax.all_gather(embeddings, "feat", axis=0, tiled=True),
        freqs,
        preferred_element_type=jnp.float32,
    )
    features = jnp.cos(mixed + phases).astype(jnp.bfloat16)
    owned_rows = lax.psum_scatter(
        jnp.dot(features, sketch, preferred_element_type=jnp.float32),
        "feat",
        scatter_dimension=0,
        tiled=True,
    )
    local_gram = jnp.dot(owned_rows.T, owned_rows, precision=lax.Precision.HIGHEST)
    gram_matrix = lax.psum(local_gram, ("rows", "feat")) / row_count
    factor = jnp.linalg.cholesky(gram_matrix)
    basis = jax.scipy.linalg.solve_triangular(factor, owned_rows.T, lower=True).T
    block_basis = lax.all_gather(basis.astype(jnp.bfloat16), "feat", axis=0, tiled=True)
    partial_value = lax.dot_general(
        block_basis, features, (((0,), (0,)), ((), ())), preferred_element_type=jnp.float32
    )
    coeffs = lax.psum(partial_value, "rows") / row_count
    return (basis, coeffs)


def per_device(embeddings, freqs, phases, sketch):
    row_count = embeddings.shape[0] * lax.axis_size("feat") * lax.axis_size("rows")
    small = row_count <= 1024 and lax.axis_size("rows") == 4 and freqs.shape[1] % 2048 == 0
    form = fused if small else general
    return form(embeddings, freqs, phases, sketch)


def solution(mesh):
    placed = (P(("rows", "feat"), None), P(None, "feat"), P("feat"), P("feat", None))
    return jax.shard_map(
        per_device,
        mesh=mesh,
        in_specs=placed,
        out_specs=(P(("rows", "feat"), None), P(None, "feat")),
        check_vma=False,
    )
```

```python
import functools

import jax
import jax.numpy as jnp
from jax import lax
from jax.experimental import pallas as pl
from jax.experimental.pallas import tpu as pltpu
from jax.sharding import PartitionSpec as P

MESH = pl.DeviceIdType.MESH
MIB = 1 << 20

INV_TAU = 0.15915494309189535
TAU_HI = 6.283203125
TAU_LO = -1.7817820414e-05
HALF_PI = 1.5707963267948966
ROUND = 12582912.0


def cosine(x):
    n = (x * INV_TAU + ROUND) - ROUND
    r = (x - n * TAU_HI) - n * TAU_LO
    w = HALF_PI - jnp.abs(r)
    z = w * w
    p = -2.3889859e-08
    p = p * z + 2.7525562e-06
    p = p * z - 1.9840874e-04
    p = p * z + 8.3333310e-03
    p = p * z - 1.6666667e-01
    return w + w * (z * p)


def peers(feats):
    r, f = lax.axis_index("rows"), lax.axis_index("feat")
    x, c = r // 2, r % 2
    sib = x * 2 + (1 - c)
    across = (1 - x) * 2 + c
    both = (1 - x) * 2 + (1 - c)
    return r, f, sib, across, both


def entry_barrier(feats):
    r, f, sib, across, _ = peers(feats)
    barrier = pltpu.get_barrier_semaphore()
    targets = [(r, lax.rem(f + k, feats)) for k in range(1, feats)]
    targets += [(sib, f), (across, f)]
    for target in targets:
        pl.semaphore_signal(barrier, inc=1, device_id=target, device_id_type=MESH)
    pl.semaphore_wait(barrier, feats + 1)


def spread(feats, rows, out_ref, send_sem, recv_sem):
    r, f, sib, across, both = peers(feats)

    def chunk(rr, ff):
        start = pl.multiple_of((rr * feats + ff) * rows, rows)
        return out_ref.at[pl.ds(start, rows)]

    sends = []

    def copy_of(rr, ff, target, slot):
        return pltpu.make_async_remote_copy(
            src_ref=chunk(rr, ff),
            dst_ref=chunk(rr, ff),
            send_sem=send_sem.at[slot],
            recv_sem=recv_sem.at[rr * feats + ff],
            device_id=target,
            device_id_type=MESH,
        )

    def send(rr, ff, target):
        copy = copy_of(rr, ff, target, len(sends))
        copy.start()
        sends.append(copy)

    def arrive(rr, ff):
        copy_of(rr, ff, (sib, f), 0).wait_recv()

    send(r, f, (across, f))
    for k in range(1, feats):
        send(r, f, (r, lax.rem(f + k, feats)))
    send(r, f, (sib, f))
    for k in range(1, feats):
        ff = lax.rem(f - k + feats, feats)
        arrive(r, ff)
        send(r, ff, (across, f))
        send(r, ff, (sib, f))
    for k in range(feats):
        ff = lax.rem(f - k + feats, feats)
        arrive(across, ff)
        send(across, ff, (sib, f))
    for k in range(feats):
        ff = lax.rem(f - k + feats, feats)
        arrive(sib, ff)
        arrive(both, ff)
    for copy in sends:
        copy.wait_send()


def gather_kernel(feats, x_ref, out_ref, send_sem, recv_sem):
    rows = x_ref.shape[0]
    r, f, *_ = peers(feats)
    entry_barrier(feats)
    start = pl.multiple_of((r * feats + f) * rows, rows)
    out_ref[pl.ds(start, rows), :] = x_ref[...]
    spread(feats, rows, out_ref, send_sem, recv_sem)


def gather_rows(x, feats, parts):
    rows, width = x.shape
    return pl.pallas_call(
        functools.partial(gather_kernel, feats),
        out_shape=jax.ShapeDtypeStruct((rows * feats * parts, width), x.dtype),
        in_specs=[pl.BlockSpec(memory_space=pltpu.VMEM)],
        out_specs=pl.BlockSpec(memory_space=pltpu.VMEM),
        scratch_shapes=[
            pltpu.SemaphoreType.DMA((feats * parts,)),
            pltpu.SemaphoreType.DMA((feats * parts,)),
        ],
        compiler_params=pltpu.CompilerParams(collective_id=0, has_side_effects=True),
    )(x)


def sum_kernel(feats, part_ref, feat_ref, out_ref, other_ref, own, pair, inbox,
               send_sem, recv_sem, pair_send, pair_recv, box_send, box_recv,
               feat_send, feat_recv):
    total = part_ref.shape[0]
    block = total // 4
    rows = block // feats
    r, f, sib, across, _ = peers(feats)
    entry_barrier(feats)

    def part(rr):
        return part_ref.at[pl.ds(pl.multiple_of(rr * block, block), block)]

    exchange = pltpu.make_async_remote_copy(
        src_ref=part(sib), dst_ref=pair, send_sem=pair_send, recv_sem=pair_recv,
        device_id=(sib, f), device_id_type=MESH,
    )
    exchange.start()
    features = pltpu.make_async_remote_copy(
        src_ref=feat_ref, dst_ref=other_ref, send_sem=feat_send, recv_sem=feat_recv,
        device_id=(sib, f), device_id_type=MESH,
    )
    exchange.wait()
    features.start()
    mine = pl.ds(pl.multiple_of(r * block, block), block)
    own[...] = part_ref[mine, :] + pair[...]

    sends = []
    for k in range(1, feats):
        ff = lax.rem(f + k, feats)
        copy = pltpu.make_async_remote_copy(
            src_ref=own.at[pl.ds(pl.multiple_of(ff * rows, rows), rows)],
            dst_ref=inbox.at[k - 1],
            send_sem=box_send.at[k - 1],
            recv_sem=box_recv.at[k - 1],
            device_id=(r, ff),
            device_id_type=MESH,
        )
        copy.start()
        sends.append(copy)
    acc = own[pl.ds(pl.multiple_of(f * rows, rows), rows), :]
    for k in range(1, feats):
        sends[k - 1].wait_recv()
        acc = acc + inbox[k - 1]
    start = pl.multiple_of((r * feats + f) * rows, rows)
    out_ref[pl.ds(start, rows), :] = acc
    spread(feats, rows, out_ref, send_sem, recv_sem)
    for copy in sends:
        copy.wait_send()
    features.wait()


def sum_and_swap(partial, features, feats):
    total, k = partial.shape
    parts = 4
    dma = pltpu.SemaphoreType.DMA
    return pl.pallas_call(
        functools.partial(sum_kernel, feats),
        out_shape=(
            jax.ShapeDtypeStruct((total, k), jnp.float32),
            jax.ShapeDtypeStruct(features.shape, features.dtype),
        ),
        in_specs=[
            pl.BlockSpec(memory_space=pltpu.VMEM),
            pl.BlockSpec(memory_space=pl.ANY),
        ],
        out_specs=(
            pl.BlockSpec(memory_space=pltpu.VMEM),
            pl.BlockSpec(memory_space=pl.ANY),
        ),
        scratch_shapes=[
            pltpu.VMEM((total // parts, k), jnp.float32),
            pltpu.VMEM((total // parts, k), jnp.float32),
            pltpu.VMEM((feats - 1, total // parts // feats, k), jnp.float32),
            dma((feats * parts,)),
            dma((feats * parts,)),
            dma(()),
            dma(()),
            dma((feats - 1,)),
            dma((feats - 1,)),
            dma(()),
            dma(()),
        ],
        compiler_params=pltpu.CompilerParams(collective_id=1, has_side_effects=True, vmem_limit_bytes=60 * MIB),
    )(partial, features)


def feature_kernel(core_ref, emb_ref, freq_ref, phase_ref, sketch_ref, feat_ref, part_ref):
    mixed = jnp.dot(emb_ref[...], freq_ref[...], preferred_element_type=jnp.float32)
    value = cosine(mixed + phase_ref[...]).astype(jnp.bfloat16)
    feat_ref[...] = value
    term = jnp.dot(value, sketch_ref[...], preferred_element_type=jnp.float32)

    @pl.when(pl.program_id(0) == 0)
    def _():
        part_ref[...] = term

    @pl.when(pl.program_id(0) > 0)
    def _():
        part_ref[...] += term


def featurize(core, emb, freqs, phases, sketch, tile=512):
    total, depth = emb.shape
    width = freqs.shape[1] // 2
    k = sketch.shape[1]
    steps = width // tile
    return pl.pallas_call(
        feature_kernel,
        grid_spec=pltpu.PrefetchScalarGridSpec(
            num_scalar_prefetch=1,
            grid=(steps,),
            in_specs=[
                pl.BlockSpec((total, depth), lambda i, c: (0, 0)),
                pl.BlockSpec((depth, tile), lambda i, c: (0, c[0] * steps + i)),
                pl.BlockSpec((1, tile), lambda i, c: (0, c[0] * steps + i)),
                pl.BlockSpec((tile, k), lambda i, c: (c[0] * steps + i, 0)),
            ],
            out_specs=[
                pl.BlockSpec((total, tile), lambda i, c: (0, i)),
                pl.BlockSpec((total, k), lambda i, c: (0, 0)),
            ],
        ),
        out_shape=(
            jax.ShapeDtypeStruct((total, width), jnp.bfloat16),
            jax.ShapeDtypeStruct((total, k), jnp.float32),
        ),
        compiler_params=pltpu.CompilerParams(vmem_limit_bytes=60 * MIB),
    )(core, emb, freqs, phases.reshape(1, -1), sketch)


GROUP = 8
BLOCK = 64
LANES = 128


def eliminate(tile, at):
    groups = BLOCK // GROUP
    m = [tile[g * GROUP:(g + 1) * GROUP, :] for g in range(groups)]
    shape = (GROUP, LANES)
    sub = lax.broadcasted_iota(jnp.int32, shape, 0)
    done = []
    for g0 in range(groups):
        base = at + g0 * GROUP
        col = [
            {g: jnp.broadcast_to(m[g][:, base + t:base + t + 1], shape) for g in range(g0, groups)}
            for t in range(GROUP)
        ]
        row = [jnp.broadcast_to(m[g0][t:t + 1, :], shape) for t in range(GROUP)]
        a = {
            (t, s): jnp.broadcast_to(col[s][g0][t:t + 1, :], shape)
            for t in range(GROUP)
            for s in range(t, GROUP)
        }
        pivots = jnp.zeros(shape, jnp.float32)
        for t in range(GROUP):
            inv = 1.0 / a[t, t]
            pivots = jnp.where(sub == t, a[t, t], pivots)
            for s in range(t + 1, GROUP):
                scaled = a[t, s] * inv
                for u in range(s, GROUP):
                    a[s, u] = a[s, u] - scaled * a[t, u]
                row[s] = row[s] - scaled * row[t]
            for g in range(g0, groups):
                f = col[t][g] * inv
                if g == g0:
                    f = jnp.where(sub > t, f, 0.0)
                for s in range(t + 1, GROUP):
                    col[s][g] = col[s][g] - f * a[t, s]
                m[g] = m[g] - f * row[t]
        done.append(m[g0] * lax.rsqrt(pivots))
    return jnp.concatenate(done, axis=0)


def factorize(scale, sk_ref, basis_ref, work):
    k = sk_ref.shape[1]
    exact = dict(preferred_element_type=jnp.float32, precision=lax.Precision.HIGHEST)
    sk = sk_ref[...]
    st = sk.T
    work[:, :k] = jnp.dot(st, sk, **exact) * scale
    work[:, k:] = st
    tile_row = lax.broadcasted_iota(jnp.int32, (BLOCK, LANES), 0)
    tile_lane = lax.broadcasted_iota(jnp.int32, (BLOCK, LANES), 1)
    for j in range(k // BLOCK):
        rows = slice(j * BLOCK, (j + 1) * BLOCK)
        edge = j * BLOCK // LANES * LANES
        at = j * BLOCK - edge
        away = BLOCK - at
        inside = (tile_lane >= at) & (tile_lane < at + BLOCK)
        eye = jnp.where(tile_lane == tile_row + away, 1.0, 0.0)
        tile = jnp.where(inside, work[rows, edge:edge + LANES], eye)
        inverse = jnp.where(inside, 0.0, eliminate(tile, at))
        panel = work[rows, edge:]
        panel = jnp.dot(inverse, jnp.concatenate([panel, panel], axis=0), **exact)
        basis_ref[rows, :] = panel[:, k - edge:]
        after = (j + 1) * BLOCK
        if after < k:
            left = after // LANES * LANES
            wide = panel[:, left - edge:]
            update = lax.dot_general(
                wide[:, :k - left], wide, (((0,), (0,)), ((), ())), **exact
            )
            work[after:, left:] = work[after:, left:] - update[after - left:, :]


def finish_kernel(scale, half, where_ref, sk_ref, own_ref, other_ref, coeff_ref, rows_ref,
                  work, basis_t, basis, half_t, feats, sem):
    step = pl.program_id(0)
    tile = coeff_ref.shape[1]
    loads = [
        pltpu.make_async_copy(
            (own_ref if i < half else other_ref).at[:, pl.ds(i % half * tile, tile)],
            feats.at[i],
            sem.at[i],
        )
        for i in range(2 * half)
    ]

    @pl.when(step == 0)
    def _():
        for load in loads:
            load.start()
        factorize(scale, sk_ref, basis_t, work)
        half_t[...] = basis_t[...].astype(jnp.bfloat16)
        basis[...] = basis_t[...].T
        rows = rows_ref.shape[0]
        rows_ref[...] = basis[pl.ds(pl.multiple_of(where_ref[1] * rows, rows), rows), :]

    for i in range(2 * half):
        @pl.when(step == i)
        def _(i=i):
            loads[i].wait()
            coeff_ref[...] = scale * jnp.dot(
                half_t[...], feats[i], preferred_element_type=jnp.float32
            )


def finish(where, sketched, own, other, rows, tile=1024):
    total, k = sketched.shape
    width = own.shape[1]
    half = width // tile
    return pl.pallas_call(
        functools.partial(finish_kernel, 1.0 / total, half),
        grid_spec=pltpu.PrefetchScalarGridSpec(
            num_scalar_prefetch=1,
            grid=(2 * half,),
            in_specs=[
                pl.BlockSpec((total, k), lambda i, c: (0, 0)),
                pl.BlockSpec(memory_space=pl.ANY),
                pl.BlockSpec(memory_space=pl.ANY),
            ],
            out_specs=[
                pl.BlockSpec(
                    (k, tile),
                    lambda i, c: (0, jnp.where(i < half, c[0], 1 - c[0]) * half + i % half),
                ),
                pl.BlockSpec((rows, k), lambda i, c: (0, 0)),
            ],
            scratch_shapes=[
                pltpu.VMEM((k, k + total), jnp.float32),
                pltpu.VMEM((k, total), jnp.float32),
                pltpu.VMEM((total, k), jnp.float32),
                pltpu.VMEM((k, total), jnp.bfloat16),
                pltpu.VMEM((2 * half, total, tile), own.dtype),
                pltpu.SemaphoreType.DMA((2 * half,)),
            ],
        ),
        out_shape=(
            jax.ShapeDtypeStruct((k, 2 * width), jnp.float32),
            jax.ShapeDtypeStruct((rows, k), jnp.float32),
        ),
        compiler_params=pltpu.CompilerParams(vmem_limit_bytes=60 * MIB),
    )(where, sketched, own, other)


def fused(embeddings, freqs, phases, sketch):
    rows_dev = embeddings.shape[0]
    feats, parts = lax.axis_size("feat"), lax.axis_size("rows")
    r, f = lax.axis_index("rows"), lax.axis_index("feat")
    where = jnp.stack([r % 2, r * feats + f]).astype(jnp.int32)
    emb = gather_rows(embeddings, feats, parts)
    own, partial = featurize(where, emb, freqs, phases, sketch)
    sketched, other = sum_and_swap(partial, own, feats)
    coeffs, basis = finish(where, sketched, own, other, rows_dev)
    return basis, coeffs


def general(embeddings, freqs, phases, sketch):
    rows_dev = embeddings.shape[0]
    row_count = rows_dev * lax.axis_size("feat") * lax.axis_size("rows")
    mixed = jnp.dot(
        lax.all_gather(embeddings, "feat", axis=0, tiled=True),
        freqs,
        preferred_element_type=jnp.float32,
    )
    features = jnp.cos(mixed + phases).astype(jnp.bfloat16)
    owned_rows = lax.psum_scatter(
        jnp.dot(features, sketch, preferred_element_type=jnp.float32),
        "feat",
        scatter_dimension=0,
        tiled=True,
    )
    local_gram = jnp.dot(owned_rows.T, owned_rows, precision=lax.Precision.HIGHEST)
    gram_matrix = lax.psum(local_gram, ("rows", "feat")) / row_count
    factor = jnp.linalg.cholesky(gram_matrix)
    basis = jax.scipy.linalg.solve_triangular(factor, owned_rows.T, lower=True).T
    block_basis = lax.all_gather(basis.astype(jnp.bfloat16), "feat", axis=0, tiled=True)
    partial_value = lax.dot_general(
        block_basis, features, (((0,), (0,)), ((), ())), preferred_element_type=jnp.float32
    )
    coeffs = lax.psum(partial_value, "rows") / row_count
    return (basis, coeffs)


def per_device(embeddings, freqs, phases, sketch):
    row_count = embeddings.shape[0] * lax.axis_size("feat") * lax.axis_size("rows")
    small = row_count <= 1024 and lax.axis_size("rows") == 4 and freqs.shape[1] % 2048 == 0
    form = fused if small else general
    return form(embeddings, freqs, phases, sketch)


def solution(mesh):
    placed = (P(("rows", "feat"), None), P(None, "feat"), P("feat"), P("feat", None))
    return jax.shard_map(
        per_device,
        mesh=mesh,
        in_specs=placed,
        out_specs=(P(("rows", "feat"), None), P(None, "feat")),
        check_vma=False,
    )
```

```python
import functools

import jax
import jax.numpy as jnp
from jax import lax
from jax.experimental import pallas as pl
from jax.experimental.pallas import tpu as pltpu
from jax.sharding import PartitionSpec as P

MESH = pl.DeviceIdType.MESH
MIB = 1 << 20

INV_TAU = 0.15915494309189535
TAU_HI = 6.283203125
TAU_LO = -1.7817820414e-05
HALF_PI = 1.5707963267948966
ROUND = 12582912.0


def cosine(x):
    n = (x * INV_TAU + ROUND) - ROUND
    r = (x - n * TAU_HI) - n * TAU_LO
    w = HALF_PI - jnp.abs(r)
    z = w * w
    p = -2.3889859e-08
    p = p * z + 2.7525562e-06
    p = p * z - 1.9840874e-04
    p = p * z + 8.3333310e-03
    p = p * z - 1.6666667e-01
    return w + w * (z * p)


def peers(feats):
    r, f = lax.axis_index("rows"), lax.axis_index("feat")
    x, c = r // 2, r % 2
    sib = x * 2 + (1 - c)
    across = (1 - x) * 2 + c
    both = (1 - x) * 2 + (1 - c)
    return r, f, sib, across, both


def entry_barrier(feats):
    r, f, sib, across, _ = peers(feats)
    barrier = pltpu.get_barrier_semaphore()
    targets = [(r, lax.rem(f + k, feats)) for k in range(1, feats)]
    targets += [(sib, f), (across, f)]
    for target in targets:
        pl.semaphore_signal(barrier, inc=1, device_id=target, device_id_type=MESH)
    pl.semaphore_wait(barrier, feats + 1)


def spread(feats, rows, out_ref, send_sem, recv_sem):
    r, f, sib, across, both = peers(feats)

    def chunk(rr, ff):
        start = pl.multiple_of((rr * feats + ff) * rows, rows)
        return out_ref.at[pl.ds(start, rows)]

    sends = []

    def copy_of(rr, ff, target, slot):
        return pltpu.make_async_remote_copy(
            src_ref=chunk(rr, ff),
            dst_ref=chunk(rr, ff),
            send_sem=send_sem.at[slot],
            recv_sem=recv_sem.at[rr * feats + ff],
            device_id=target,
            device_id_type=MESH,
        )

    def send(rr, ff, target):
        copy = copy_of(rr, ff, target, len(sends))
        copy.start()
        sends.append(copy)

    def arrive(rr, ff):
        copy_of(rr, ff, (sib, f), 0).wait_recv()

    send(r, f, (across, f))
    for k in range(1, feats):
        send(r, f, (r, lax.rem(f + k, feats)))
    send(r, f, (sib, f))
    for k in range(1, feats):
        ff = lax.rem(f - k + feats, feats)
        arrive(r, ff)
        send(r, ff, (across, f))
        send(r, ff, (sib, f))
    for k in range(feats):
        ff = lax.rem(f - k + feats, feats)
        arrive(across, ff)
        send(across, ff, (sib, f))
    for k in range(feats):
        ff = lax.rem(f - k + feats, feats)
        arrive(sib, ff)
        arrive(both, ff)
    for copy in sends:
        copy.wait_send()


def gather_kernel(feats, x_ref, out_ref, send_sem, recv_sem):
    rows = x_ref.shape[0]
    r, f, *_ = peers(feats)
    entry_barrier(feats)
    start = pl.multiple_of((r * feats + f) * rows, rows)
    out_ref[pl.ds(start, rows), :] = x_ref[...]
    spread(feats, rows, out_ref, send_sem, recv_sem)


def gather_rows(x, feats, parts):
    rows, width = x.shape
    return pl.pallas_call(
        functools.partial(gather_kernel, feats),
        out_shape=jax.ShapeDtypeStruct((rows * feats * parts, width), x.dtype),
        in_specs=[pl.BlockSpec(memory_space=pltpu.VMEM)],
        out_specs=pl.BlockSpec(memory_space=pltpu.VMEM),
        scratch_shapes=[
            pltpu.SemaphoreType.DMA((feats * parts,)),
            pltpu.SemaphoreType.DMA((feats * parts,)),
        ],
        compiler_params=pltpu.CompilerParams(collective_id=0, has_side_effects=True),
    )(x)


def sum_kernel(feats, part_ref, feat_ref, out_ref, other_ref, own, pair, inbox,
               send_sem, recv_sem, pair_send, pair_recv, box_send, box_recv,
               feat_send, feat_recv):
    total = part_ref.shape[0]
    block = total // 4
    rows = block // feats
    r, f, sib, across, _ = peers(feats)
    entry_barrier(feats)

    def part(rr):
        return part_ref.at[pl.ds(pl.multiple_of(rr * block, block), block)]

    exchange = pltpu.make_async_remote_copy(
        src_ref=part(sib), dst_ref=pair, send_sem=pair_send, recv_sem=pair_recv,
        device_id=(sib, f), device_id_type=MESH,
    )
    exchange.start()
    features = pltpu.make_async_remote_copy(
        src_ref=feat_ref, dst_ref=other_ref, send_sem=feat_send, recv_sem=feat_recv,
        device_id=(sib, f), device_id_type=MESH,
    )
    exchange.wait()
    features.start()
    mine = pl.ds(pl.multiple_of(r * block, block), block)
    own[...] = part_ref[mine, :] + pair[...]

    sends = []
    for k in range(1, feats):
        ff = lax.rem(f + k, feats)
        copy = pltpu.make_async_remote_copy(
            src_ref=own.at[pl.ds(pl.multiple_of(ff * rows, rows), rows)],
            dst_ref=inbox.at[k - 1],
            send_sem=box_send.at[k - 1],
            recv_sem=box_recv.at[k - 1],
            device_id=(r, ff),
            device_id_type=MESH,
        )
        copy.start()
        sends.append(copy)
    acc = own[pl.ds(pl.multiple_of(f * rows, rows), rows), :]
    for k in range(1, feats):
        sends[k - 1].wait_recv()
        acc = acc + inbox[k - 1]
    start = pl.multiple_of((r * feats + f) * rows, rows)
    out_ref[pl.ds(start, rows), :] = acc
    spread(feats, rows, out_ref, send_sem, recv_sem)
    for copy in sends:
        copy.wait_send()
    features.wait()


def sum_and_swap(partial, features, feats):
    total, k = partial.shape
    parts = 4
    dma = pltpu.SemaphoreType.DMA
    return pl.pallas_call(
        functools.partial(sum_kernel, feats),
        out_shape=(
            jax.ShapeDtypeStruct((total, k), jnp.float32),
            jax.ShapeDtypeStruct(features.shape, features.dtype),
        ),
        in_specs=[
            pl.BlockSpec(memory_space=pltpu.VMEM),
            pl.BlockSpec(memory_space=pl.ANY),
        ],
        out_specs=(
            pl.BlockSpec(memory_space=pltpu.VMEM),
            pl.BlockSpec(memory_space=pl.ANY),
        ),
        scratch_shapes=[
            pltpu.VMEM((total // parts, k), jnp.float32),
            pltpu.VMEM((total // parts, k), jnp.float32),
            pltpu.VMEM((feats - 1, total // parts // feats, k), jnp.float32),
            dma((feats * parts,)),
            dma((feats * parts,)),
            dma(()),
            dma(()),
            dma((feats - 1,)),
            dma((feats - 1,)),
            dma(()),
            dma(()),
        ],
        compiler_params=pltpu.CompilerParams(collective_id=1, has_side_effects=True, vmem_limit_bytes=60 * MIB),
    )(partial, features)


def feature_kernel(core_ref, emb_ref, freq_ref, phase_ref, sketch_ref, feat_ref, part_ref):
    first = pl.program_id(0) == 0
    piece = emb_ref.shape[0] // 2
    for h in range(2):
        rows = slice(h * piece, (h + 1) * piece)
        mixed = jnp.dot(emb_ref[rows, :], freq_ref[...], preferred_element_type=jnp.float32)
        value = cosine(mixed + phase_ref[...]).astype(jnp.bfloat16)
        feat_ref[rows, :] = value
        term = jnp.dot(value, sketch_ref[...], preferred_element_type=jnp.float32)
        part_ref[rows, :] = jnp.where(first, 0.0, part_ref[rows, :]) + term


def featurize(core, emb, freqs, phases, sketch, tile=512):
    total, depth = emb.shape
    width = freqs.shape[1] // 2
    k = sketch.shape[1]
    steps = width // tile
    return pl.pallas_call(
        feature_kernel,
        grid_spec=pltpu.PrefetchScalarGridSpec(
            num_scalar_prefetch=1,
            grid=(steps,),
            in_specs=[
                pl.BlockSpec((total, depth), lambda i, c: (0, 0)),
                pl.BlockSpec((depth, tile), lambda i, c: (0, c[0] * steps + i)),
                pl.BlockSpec((1, tile), lambda i, c: (0, c[0] * steps + i)),
                pl.BlockSpec((tile, k), lambda i, c: (c[0] * steps + i, 0)),
            ],
            out_specs=[
                pl.BlockSpec((total, tile), lambda i, c: (0, i)),
                pl.BlockSpec((total, k), lambda i, c: (0, 0)),
            ],
        ),
        out_shape=(
            jax.ShapeDtypeStruct((total, width), jnp.bfloat16),
            jax.ShapeDtypeStruct((total, k), jnp.float32),
        ),
        compiler_params=pltpu.CompilerParams(vmem_limit_bytes=60 * MIB),
    )(core, emb, freqs, phases.reshape(1, -1), sketch)


GROUP = 8
BLOCK = 64
LANES = 128


def eliminate(tile, at):
    groups = BLOCK // GROUP
    m = [tile[g * GROUP:(g + 1) * GROUP, :] for g in range(groups)]
    shape = (GROUP, LANES)
    sub = lax.broadcasted_iota(jnp.int32, shape, 0)
    done = []
    for g0 in range(groups):
        base = at + g0 * GROUP
        col = [
            {g: jnp.broadcast_to(m[g][:, base + t:base + t + 1], shape) for g in range(g0, groups)}
            for t in range(GROUP)
        ]
        row = [jnp.broadcast_to(m[g0][t:t + 1, :], shape) for t in range(GROUP)]
        a = {
            (t, s): jnp.broadcast_to(col[s][g0][t:t + 1, :], shape)
            for t in range(GROUP)
            for s in range(t, GROUP)
        }
        pivots = jnp.zeros(shape, jnp.float32)
        for t in range(GROUP):
            inv = 1.0 / a[t, t]
            pivots = jnp.where(sub == t, a[t, t], pivots)
            for s in range(t + 1, GROUP):
                scaled = a[t, s] * inv
                for u in range(s, GROUP):
                    a[s, u] = a[s, u] - scaled * a[t, u]
                row[s] = row[s] - scaled * row[t]
            for g in range(g0, groups):
                f = col[t][g] * inv
                if g == g0:
                    f = jnp.where(sub > t, f, 0.0)
                for s in range(t + 1, GROUP):
                    col[s][g] = col[s][g] - f * a[t, s]
                m[g] = m[g] - f * row[t]
        done.append(m[g0] * lax.rsqrt(pivots))
    return jnp.concatenate(done, axis=0)


def factorize(scale, sk_ref, basis_ref, work):
    k = sk_ref.shape[1]
    exact = dict(preferred_element_type=jnp.float32, precision=lax.Precision.HIGHEST)
    sk = sk_ref[...]
    st = sk.T
    work[:, :k] = jnp.dot(st, sk, **exact) * scale
    work[:, k:] = st
    tile_row = lax.broadcasted_iota(jnp.int32, (BLOCK, LANES), 0)
    tile_lane = lax.broadcasted_iota(jnp.int32, (BLOCK, LANES), 1)
    for j in range(k // BLOCK):
        rows = slice(j * BLOCK, (j + 1) * BLOCK)
        edge = j * BLOCK // LANES * LANES
        at = j * BLOCK - edge
        away = BLOCK - at
        inside = (tile_lane >= at) & (tile_lane < at + BLOCK)
        eye = jnp.where(tile_lane == tile_row + away, 1.0, 0.0)
        tile = jnp.where(inside, work[rows, edge:edge + LANES], eye)
        inverse = jnp.where(inside, 0.0, eliminate(tile, at))
        panel = work[rows, edge:]
        panel = jnp.dot(inverse, jnp.concatenate([panel, panel], axis=0), **exact)
        basis_ref[rows, :] = panel[:, k - edge:]
        after = (j + 1) * BLOCK
        if after < k:
            left = after // LANES * LANES
            wide = panel[:, left - edge:]
            update = lax.dot_general(
                wide[:, :k - left], wide, (((0,), (0,)), ((), ())), **exact
            )
            work[after:, left:] = work[after:, left:] - update[after - left:, :]


def finish_kernel(scale, half, core_ref, place_ref, sk_ref, own_ref, other_ref, coeff_ref,
                  rows_ref, work, basis_t, basis, half_t, feats, out, sem, out_sem):
    tile = out.shape[2]
    core = core_ref[0]
    loads, stores = [], []
    for i in range(2 * half):
        loads.append(pltpu.make_async_copy(
            (own_ref if i < half else other_ref).at[:, pl.ds(i % half * tile, tile)],
            feats.at[i],
            sem.at[i],
        ))
        block = (core if i < half else 1 - core) * half + i % half
        stores.append(pltpu.make_async_copy(
            out.at[i],
            coeff_ref.at[:, pl.ds(pl.multiple_of(block * tile, tile), tile)],
            out_sem.at[i],
        ))
    for load in loads:
        load.start()
    factorize(scale, sk_ref, basis_t, work)
    half_t[...] = basis_t[...].astype(jnp.bfloat16)
    for i in range(2 * half):
        loads[i].wait()
        out[i] = scale * jnp.dot(half_t[...], feats[i], preferred_element_type=jnp.float32)
        stores[i].start()
    basis[...] = basis_t[...].T
    rows = rows_ref.shape[0]
    rows_ref[...] = basis[pl.ds(pl.multiple_of(place_ref[0] * rows, rows), rows), :]
    for store in stores:
        store.wait()


def finish(core, place, sketched, own, other, rows, tile=1024):
    total, k = sketched.shape
    width = own.shape[1]
    half = width // tile
    return pl.pallas_call(
        functools.partial(finish_kernel, 1.0 / total, half),
        in_specs=[
            pl.BlockSpec(memory_space=pltpu.SMEM),
            pl.BlockSpec(memory_space=pltpu.SMEM),
            pl.BlockSpec(memory_space=pltpu.VMEM),
            pl.BlockSpec(memory_space=pl.ANY),
            pl.BlockSpec(memory_space=pl.ANY),
        ],
        out_specs=[
            pl.BlockSpec(memory_space=pl.ANY),
            pl.BlockSpec(memory_space=pltpu.VMEM),
        ],
        scratch_shapes=[
            pltpu.VMEM((k, k + total), jnp.float32),
            pltpu.VMEM((k, total), jnp.float32),
            pltpu.VMEM((total, k), jnp.float32),
            pltpu.VMEM((k, total), jnp.bfloat16),
            pltpu.VMEM((2 * half, total, tile), own.dtype),
            pltpu.VMEM((2 * half, k, tile), jnp.float32),
            pltpu.SemaphoreType.DMA((2 * half,)),
            pltpu.SemaphoreType.DMA((2 * half,)),
        ],
        out_shape=(
            jax.ShapeDtypeStruct((k, 2 * width), jnp.float32),
            jax.ShapeDtypeStruct((rows, k), jnp.float32),
        ),
        compiler_params=pltpu.CompilerParams(vmem_limit_bytes=60 * MIB),
    )(core, place, sketched, own, other)


def fused(embeddings, freqs, phases, sketch):
    rows_dev = embeddings.shape[0]
    feats, parts = lax.axis_size("feat"), lax.axis_size("rows")
    r, f = lax.axis_index("rows"), lax.axis_index("feat")
    core = jnp.reshape(r % 2, (1,)).astype(jnp.int32)
    place = jnp.reshape(r * feats + f, (1,)).astype(jnp.int32)
    emb = gather_rows(embeddings, feats, parts)
    own, partial = featurize(core, emb, freqs, phases, sketch)
    sketched, other = sum_and_swap(partial, own, feats)
    coeffs, basis = finish(core, place, sketched, own, other, rows_dev)
    return basis, coeffs


def general(embeddings, freqs, phases, sketch):
    rows_dev = embeddings.shape[0]
    row_count = rows_dev * lax.axis_size("feat") * lax.axis_size("rows")
    mixed = jnp.dot(
        lax.all_gather(embeddings, "feat", axis=0, tiled=True),
        freqs,
        preferred_element_type=jnp.float32,
    )
    features = jnp.cos(mixed + phases).astype(jnp.bfloat16)
    owned_rows = lax.psum_scatter(
        jnp.dot(features, sketch, preferred_element_type=jnp.float32),
        "feat",
        scatter_dimension=0,
        tiled=True,
    )
    local_gram = jnp.dot(owned_rows.T, owned_rows, precision=lax.Precision.HIGHEST)
    gram_matrix = lax.psum(local_gram, ("rows", "feat")) / row_count
    factor = jnp.linalg.cholesky(gram_matrix)
    basis = jax.scipy.linalg.solve_triangular(factor, owned_rows.T, lower=True).T
    block_basis = lax.all_gather(basis.astype(jnp.bfloat16), "feat", axis=0, tiled=True)
    partial_value = lax.dot_general(
        block_basis, features, (((0,), (0,)), ((), ())), preferred_element_type=jnp.float32
    )
    coeffs = lax.psum(partial_value, "rows") / row_count
    return (basis, coeffs)


def per_device(embeddings, freqs, phases, sketch):
    row_count = embeddings.shape[0] * lax.axis_size("feat") * lax.axis_size("rows")
    small = row_count <= 1024 and lax.axis_size("rows") == 4 and freqs.shape[1] % 2048 == 0
    form = fused if small else general
    return form(embeddings, freqs, phases, sketch)


def solution(mesh):
    placed = (P(("rows", "feat"), None), P(None, "feat"), P("feat"), P("feat", None))
    return jax.shard_map(
        per_device,
        mesh=mesh,
        in_specs=placed,
        out_specs=(P(("rows", "feat"), None), P(None, "feat")),
        check_vma=False,
    )
```
